32 devices in a mesh: group: 4 (over y, x), head: 4 (over z), seq: 2 (over core).
Axes of the slice: x: 2, y: 2, z: 4, core: 2. Of those that a mesh axis runs over, the one named last changes fastest.
Arguments:
- prefix_q: bfloat16 [1536, 4096], P(('group', 'seq'), 'head'), may hold values from -32 to 32
- prefix_k: bfloat16 [1536, 1024], P(('group', 'seq'), 'head'), may hold values from -6 to 6
- prefix_v: bfloat16 [1536, 1024], P(('group', 'seq'), 'head'), may hold values from -6 to 6
- resp_q: bfloat16 [4096, 4096], P(('group', 'seq'), 'head'), may hold values from -32 to 32
- resp_k: bfloat16 [4096, 1024], P(('group', 'seq'), 'head'), may hold values from -6 to 6
- resp_v: bfloat16 [4096, 1024], P(('group', 'seq'), 'head'), may hold values from -6 to 6
- resp_len: int32 [8], P(('group', 'seq')), may hold values from 64 to 512
- resp_prompt: int32 [8], P(('group', 'seq')), may hold values from 0 to 1
- out_weight: bfloat16 [4096, 4096], P('head'), may hold values from -0.09375 to 0.09375
- prefix_grad: bfloat16 [1536, 4096], P(('group', 'seq'), 'head'), may hold values from -6 to 6
- resp_grad: bfloat16 [4096, 4096], P(('group', 'seq'), 'head'), may hold values from -6 to 6
Outputs:
- prefix_out: bfloat16 [1536, 4096], P(('group', 'seq'), 'head')
- resp_out: bfloat16 [4096, 4096], P(('group', 'seq'), 'head')
- d_prefix_q: bfloat16 [1536, 4096], P(('group', 'seq'), 'head')
- d_prefix_k: bfloat16 [1536, 1024], P(('group', 'seq'), 'head')
- d_prefix_v: bfloat16 [1536, 1024], P(('group', 'seq'), 'head')
- d_resp_q: bfloat16 [4096, 4096], P(('group', 'seq'), 'head')
- d_resp_k: bfloat16 [4096, 1024], P(('group', 'seq'), 'head')
- d_resp_v: bfloat16 [4096, 1024], P(('group', 'seq'), 'head')
- d_out_weight: float32 [4096, 4096], P('head')
The draws below stay inside these ranges and needn't reach their ends.
Inputs may be any that keep to these rules, and one draw needn't show every extreme that they name: Rows from resp_len to 512 of a response slot are padding.
All inputs are finite; a program needn't handle non-finite values.
Results may differ from the reference program's by a relative error of at most 0.017.
Values may be sent and summed in bfloat16 or wider, within the bound.
A program may use at most 192 MiB of HBM per device.

```python
import jax
import jax.numpy as jnp
from jax import lax

D = 4096
QH = 32
KVH = 8
HD = 128
RMAX = 512
PREFIX = 1536
RESP = 8


def drawn_rows(key, salt, rows, heads):
    base = jnp.clip(jax.random.normal(jax.random.fold_in(key, salt), (rows, heads * HD), jnp.float32), -6.0, 6.0)
    return base


def draw_prefix_q(key, part):
    return drawn_rows(key, 101, PREFIX, QH).astype(jnp.bfloat16)


def draw_resp_q(key, part):
    return drawn_rows(key, 202, RESP * RMAX, QH).astype(jnp.bfloat16)


def draw_prefix_k(key, part):
    return drawn_rows(key, 303, PREFIX, KVH).astype(jnp.bfloat16)


def set_ends(values, stream_key, low, top_value):
    longest = values.shape.index(max(values.shape))
    spots = []
    for shift in (0, 1):
        where = [jax.random.randint(jax.random.fold_in(stream_key, axis), (), 0, length) for axis, length in enumerate(values.shape)]
        where[longest] = (where[longest] + shift) % values.shape[longest]
        spots.append(tuple(where))
    return values.at[spots[0]].set(low).at[spots[1]].set(top_value)


def block_scale(key, dims, split, smallest, top_value):
    gain = 1.0
    for axis_at, blocks in split:
        steps = jax.random.uniform(jax.random.fold_in(jax.random.fold_in(key, 6), axis_at), (blocks,), jnp.float32, smallest / len(split), top_value / len(split))
        gain = gain * jnp.repeat(jnp.exp(steps), dims[axis_at] // blocks).reshape((-1,) + (1,) * (len(dims) - 1 - axis_at))
    return gain


def normal_values(key, shape, scale, bound, shards=(), held_as=jnp.bfloat16):
    result = scale * jax.random.normal(key, shape, jnp.float32)
    if shards:
        result = result * block_scale(key, shape, shards, -0.22, 0.18)
    return jnp.clip(result, -bound, bound).astype(held_as)


def setup_inputs(seed: int = 0) -> dict:
    splits = jax.random.split(jax.random.key(seed), 12)
    prefix_q = draw_prefix_q(jax.random.fold_in(splits[11], 71), 0)
    prefix_k = draw_prefix_k(jax.random.fold_in(splits[11], 71), 0)
    prefix_v = normal_values(splits[2], (PREFIX, KVH * HD), 1.0, 6.0, ((0, 8), (1, 4)))
    resp_q = draw_resp_q(jax.random.fold_in(splits[11], 71), 0)
    resp_k = normal_values(splits[4], (RESP * RMAX, KVH * HD), 1.0, 6.0, ((0, 8), (1, 4)))
    resp_v = normal_values(splits[5], (RESP * RMAX, KVH * HD), 1.0, 6.0, ((0, 8), (1, 4)))
    resp_len = set_ends(jax.random.randint(splits[6], (RESP,), RMAX // 8, RMAX + 1), jax.random.fold_in(splits[6], 1), RMAX // 8, RMAX).astype(jnp.int32)
    resp_prompt = set_ends(jax.random.randint(splits[7], (RESP,), 0, 2), jax.random.fold_in(splits[7], 1), 0, 1).astype(jnp.int32)
    out_weight = normal_values(splits[8], (QH * HD, D), (QH * HD) ** -0.5, 0.09375, ((0, 4),))
    prefix_grad = normal_values(splits[9], (PREFIX, D), 1.0, 6.0, ((0, 8), (1, 4)))
    resp_grad = normal_values(splits[10], (RESP * RMAX, D), 1.0, 6.0, ((0, 8), (1, 4)))
    return {"prefix_q": prefix_q, "prefix_k": prefix_k, "prefix_v": prefix_v, "resp_q": resp_q, "resp_k": resp_k, "resp_v": resp_v, "resp_len": resp_len, "resp_prompt": resp_prompt, "out_weight": out_weight, "prefix_grad": prefix_grad, "resp_grad": resp_grad}


masked_value = -1e30


def rounded(value):
    return lax.optimization_barrier(value.astype(jnp.bfloat16)).astype(jnp.float32)


def attend(queries, keys, values, seen, dout, valid):
    scale = HD ** -0.5
    highest = lax.Precision.HIGHEST
    raw = jnp.einsum("brgd,bnd->bgrn", queries, keys, precision=highest) * scale
    scores = jnp.where(seen[:, None], raw, masked_value)
    top = jnp.max(scores, -1, keepdims=True)
    lse = top + jnp.log(jnp.sum(jnp.exp(scores - top), -1, keepdims=True))
    prob = jnp.exp(scores - lse)
    weights = rounded(prob)
    heads_out = rounded(jnp.einsum("bgrn,bnd->brgd", weights, values, precision=highest) * valid[:, :, None, None])
    delta = jnp.transpose(jnp.sum(dout * heads_out, -1), (0, 2, 1))
    dprob = jnp.einsum("brgd,bnd->bgrn", dout, values, precision=highest)
    dscore = rounded(prob * (dprob - delta[..., None]))
    dquery = jnp.einsum("bgrn,bnd->brgd", dscore, keys, precision=highest)
    dkey = jnp.einsum("bgrn,brgd->bnd", dscore, queries, precision=highest)
    dvalue = jnp.einsum("bgrn,brgd->bnd", weights, dout, precision=highest)
    return heads_out, dquery, dkey, dvalue


def reference(prefix_q, prefix_k, prefix_v, resp_q, resp_k, resp_v, resp_len, resp_prompt, out_weight, prefix_grad, resp_grad):
    group_q = QH // KVH
    prompt_len = PREFIX // 2
    scale = HD ** -0.5
    highest = lax.Precision.HIGHEST
    live = (jnp.arange(RMAX, dtype=jnp.int32)[None, :] < resp_len[:, None]).astype(jnp.float32)
    live_rows = live.reshape(RESP * RMAX)
    pq = prefix_q.astype(jnp.float32).reshape(2, prompt_len, KVH, group_q, HD).transpose(2, 0, 1, 3, 4)
    pk = prefix_k.astype(jnp.float32).reshape(2, prompt_len, KVH, HD).transpose(2, 0, 1, 3)
    pv = prefix_v.astype(jnp.float32).reshape(2, prompt_len, KVH, HD).transpose(2, 0, 1, 3)
    rq = resp_q.astype(jnp.float32).reshape(RESP, RMAX, KVH, group_q, HD).transpose(2, 0, 1, 3, 4)
    rk = resp_k.astype(jnp.float32).reshape(RESP, RMAX, KVH, HD).transpose(2, 0, 1, 3)
    rv = resp_v.astype(jnp.float32).reshape(RESP, RMAX, KVH, HD).transpose(2, 0, 1, 3)
    wo = out_weight.reshape(KVH, group_q * HD, D)
    causal = jnp.arange(prompt_len)[:, None] >= jnp.arange(prompt_len)[None, :]
    self_causal = jnp.arange(RMAX)[:, None] >= jnp.arange(RMAX)[None, :]
    resp_seen = jnp.concatenate([jnp.ones((RMAX, prompt_len), bool), self_causal], 1)
    chosen = (resp_prompt[None, :] == jnp.arange(2, dtype=jnp.int32)[:, None]).astype(jnp.float32)

    def per_head(inputs):
        wo_h, pq_h, pk_h, pv_h, rq_h, rk_h, rv_h = inputs
        dout_p = rounded(jnp.dot(prefix_grad, wo_h.T, preferred_element_type=jnp.float32))
        dout_p = dout_p.reshape(2, prompt_len, group_q, HD)
        dout_r = rounded(jnp.dot(resp_grad, wo_h.T, preferred_element_type=jnp.float32) * live_rows[:, None])
        dout_r = dout_r.reshape(RESP, RMAX, group_q, HD)
        out_p, dq_p, dk_p, dv_p = attend(pq_h, pk_h, pv_h, causal[None], dout_p, jnp.ones((2, prompt_len), jnp.float32))
        keys = jnp.concatenate([pk_h[resp_prompt], rk_h], 1)
        values = jnp.concatenate([pv_h[resp_prompt], rv_h], 1)
        out_r, dq_r, dk_r, dv_r = attend(rq_h, keys, values, resp_seen[None], dout_r, live)
        dk_p = dk_p + jnp.einsum("pb,bnd->pnd", chosen, dk_r[:, :prompt_len], precision=highest)
        dv_p = dv_p + jnp.einsum("pb,bnd->pnd", chosen, dv_r[:, :prompt_len], precision=highest)
        return out_p, out_r, dq_p, dq_r, dk_p, dv_p, dk_r[:, prompt_len:], dv_r[:, prompt_len:]

    out_p, out_r, dq_p, dq_r, dk_p, dv_p, dk_r, dv_r = lax.map(per_head, (wo, pq, pk, pv, rq, rk, rv))
    attn_p = out_p.transpose(1, 2, 0, 3, 4).reshape(PREFIX, QH * HD).astype(jnp.bfloat16)
    attn_r = out_r.transpose(1, 2, 0, 3, 4).reshape(RESP * RMAX, QH * HD).astype(jnp.bfloat16)
    prefix_out = jnp.dot(attn_p, out_weight, preferred_element_type=jnp.float32).astype(jnp.bfloat16)
    resp_out = jnp.dot(attn_r, out_weight, preferred_element_type=jnp.float32).astype(jnp.bfloat16)
    weight_grad = jnp.dot(attn_p.T, prefix_grad, preferred_element_type=jnp.float32)
    weight_grad = weight_grad + jnp.dot(attn_r.T, resp_grad, preferred_element_type=jnp.float32)
    d_prefix_q = (dq_p * scale).transpose(1, 2, 0, 3, 4).reshape(PREFIX, QH * HD).astype(jnp.bfloat16)
    d_resp_q = (dq_r * scale).transpose(1, 2, 0, 3, 4).reshape(RESP * RMAX, QH * HD).astype(jnp.bfloat16)
    d_prefix_k = (dk_p * scale).transpose(1, 2, 0, 3).reshape(PREFIX, KVH * HD).astype(jnp.bfloat16)
    d_prefix_v = dv_p.transpose(1, 2, 0, 3).reshape(PREFIX, KVH * HD).astype(jnp.bfloat16)
    d_resp_k = (dk_r * scale).transpose(1, 2, 0, 3).reshape(RESP * RMAX, KVH * HD).astype(jnp.bfloat16)
    d_resp_v = dv_r.transpose(1, 2, 0, 3).reshape(RESP * RMAX, KVH * HD).astype(jnp.bfloat16)
    return (prefix_out, resp_out, d_prefix_q, d_prefix_k, d_prefix_v, d_resp_q, d_resp_k, d_resp_v, weight_grad)
```

```python
import functools

import jax
import jax.numpy as jnp
from jax import lax
from jax.experimental import pallas as pl
from jax.experimental.pallas import tpu as pltpu
from jax.sharding import PartitionSpec as P

HD = 128
TOKENS = ("group", "seq")
SCALE = HD ** (-0.5)
LOG2E = 1.4426950408889634
MASKED = -1e30


def nt(a, b):
    return lax.dot_general(a, b, (((1,), (1,)), ((), ())), preferred_element_type=jnp.float32)


def tn(a, b):
    return lax.dot_general(a, b, (((0,), (0,)), ((), ())), preferred_element_type=jnp.float32)


def nn(a, b):
    return jnp.dot(a, b, preferred_element_type=jnp.float32)


def causal_t(scores, offset):
    key = lax.broadcasted_iota(jnp.int32, scores.shape, 0)
    row = lax.broadcasted_iota(jnp.int32, scores.shape, 1)
    return jnp.where(key <= row + offset, scores, MASKED)


def forward_kernel(info, pq, rq, pk, pv, sk, sv, rk, rv, attn, lse):
    rows_p = pq.shape[0]
    factor = SCALE * LOG2E
    s = causal_t(nt(pk[...], pq[...]), info[0])
    top = jnp.max(s, 0, keepdims=True)
    p = jnp.exp2((s - top) * factor)
    total = jnp.sum(p, 0, keepdims=True)
    out = tn(pv[...], p.astype(jnp.bfloat16)) / total
    attn[:rows_p] = out.T.astype(jnp.bfloat16)
    lse[0, :, :rows_p] = top * factor + jnp.log2(total)
    a = nt(sk[...], rq[...])
    b = causal_t(nt(rk[...], rq[...]), 0)
    top = jnp.maximum(jnp.max(a, 0, keepdims=True), jnp.max(b, 0, keepdims=True))
    pa = jnp.exp2((a - top) * factor)
    pb = jnp.exp2((b - top) * factor)
    total = jnp.sum(pa, 0, keepdims=True) + jnp.sum(pb, 0, keepdims=True)
    out = tn(sv[...], pa.astype(jnp.bfloat16)) + tn(rv[...], pb.astype(jnp.bfloat16))
    live = lax.broadcasted_iota(jnp.int32, total.shape, 1) < info[1]
    out = out * jnp.where(live, 1.0 / total, 0.0)
    attn[rows_p:] = out.T.astype(jnp.bfloat16)
    lse[0, :, rows_p:] = top * factor + jnp.log2(total)


def row_sums_t(x):
    high = x.astype(jnp.bfloat16)
    low = (x - high.astype(jnp.float32)).astype(jnp.bfloat16)
    ones = jnp.ones((8, x.shape[1]), jnp.bfloat16)
    return (nt(ones, high) + nt(ones, low))[:1]


def backward_kernel(
    q_group, info, pq, rq, pk, pv, sk, sv, rk, rv, attn, dout, lse,
    dpq, drq, dpk, dpv, dsk, dsv, drk, drv,
    apk, apv, ask, asv, ark, arv,
):
    rows_p = pq.shape[0]
    factor = SCALE * LOG2E
    step = lax.rem(pl.program_id(0), q_group)
    accs = (apk, apv, ask, asv, ark, arv)

    @pl.when(step == 0)
    def _():
        for acc in accs:
            acc[...] = jnp.zeros_like(acc)

    delta = row_sums_t(dout[...].astype(jnp.float32) * attn[...].astype(jnp.float32))

    def piece(q, do, k, v, lse_row, delta_row, offset, acc_k, acc_v):
        s = nt(k, q)
        if offset is not None:
            s = causal_t(s, offset)
        p = jnp.exp2(s * factor - lse_row)
        ds = (p * (nt(v, do) - delta_row)).astype(jnp.bfloat16)
        acc_k[...] += nn(ds, q)
        acc_v[...] += nn(p.astype(jnp.bfloat16), do)
        return tn(k, ds)

    dq = piece(pq[...], dout[:rows_p], pk[...], pv[...], lse[0, :, :rows_p], delta[:, :rows_p],
               info[0], apk, apv)
    dpq[...] = (dq * SCALE).T.astype(jnp.bfloat16)
    q, do, lr, dr = rq[...], dout[rows_p:], lse[0, :, rows_p:], delta[:, rows_p:]
    dq = piece(q, do, sk[...], sv[...], lr, dr, None, ask, asv)
    dq = dq + piece(q, do, rk[...], rv[...], lr, dr, 0, ark, arv)
    drq[...] = (dq * SCALE).T.astype(jnp.bfloat16)

    @pl.when(step == q_group - 1)
    def _():
        dpk[...] = apk[...] * SCALE
        dpv[...] = apv[...]
        dsk[...] = ask[...] * SCALE
        dsv[...] = asv[...]
        drk[...] = (ark[...] * SCALE).astype(jnp.bfloat16)
        drv[...] = arv[...].astype(jnp.bfloat16)


def on_device(
    prefix_q, prefix_k, prefix_v, resp_q, resp_k, resp_v,
    resp_len, resp_prompt, out_weight, prefix_grad, resp_grad,
):
    n = lax.axis_size("head")
    z = lax.axis_index("head")
    shards = lax.axis_size(TOKENS)
    me = lax.axis_index(TOKENS)
    rows_p, rows_r = prefix_q.shape[0], resp_q.shape[0]
    rows = rows_p + rows_r
    kv = prefix_k.shape[1]
    q_group = prefix_q.shape[1] // kv
    heads = prefix_q.shape[1] // HD
    prompt_len = rows_p * shards // 2
    share = prefix_grad.shape[1]
    ring = [(i, (i + 1) % n) for i in range(n)]
    bf16, f32 = jnp.bfloat16, jnp.float32

    shares = [jnp.concatenate([prefix_grad, resp_grad], 0)]
    for _ in range(n - 1):
        shares.append(lax.ppermute(shares[-1], "head", ring))

    def weight_cut(r):
        return lax.dynamic_slice_in_dim(out_weight, lax.rem(z - r + n, n) * share, share, 1)

    cuts = [weight_cut(r) for r in range(n)]

    both = lax.all_gather(jnp.concatenate([prefix_k, prefix_v], 1), TOKENS, axis=0, tiled=True)
    own = me * rows_p // prompt_len
    own_kv = lax.dynamic_slice_in_dim(both, own * prompt_len, prompt_len, 0)
    seen_kv = lax.dynamic_slice_in_dim(both, resp_prompt[0] * prompt_len, prompt_len, 0)
    info = jnp.stack([me * rows_p - own * prompt_len, resp_len[0]]).astype(jnp.int32)

    smem = pl.BlockSpec(memory_space=pltpu.SMEM)
    kv_heads = kv // HD

    def q_spec(count):
        return pl.BlockSpec((count, HD), lambda i: (0, i))

    def k_spec(count, shift=0):
        return pl.BlockSpec((count, HD), lambda i: (0, i // q_group + shift))

    kv_specs = [
        q_spec(rows_p), q_spec(rows_r),
        k_spec(prompt_len), k_spec(prompt_len, kv_heads),
        k_spec(prompt_len), k_spec(prompt_len, kv_heads),
        k_spec(rows_r), k_spec(rows_r),
    ]
    kv_args = (prefix_q, resp_q, own_kv, own_kv, seen_kv, seen_kv, resp_k, resp_v)
    lse_spec = pl.BlockSpec((1, 1, rows), lambda i: (i, 0, 0))
    pairs = heads * (rows_p * prompt_len + rows_r * (prompt_len + rows_r))
    params = pltpu.CompilerParams(
        dimension_semantics=("arbitrary",), vmem_limit_bytes=48 * 2**20
    )
    attn, lse = pl.pallas_call(
        forward_kernel,
        grid=(heads,),
        in_specs=[smem] + kv_specs,
        out_specs=[q_spec(rows), lse_spec],
        out_shape=[
            jax.ShapeDtypeStruct((rows, heads * HD), bf16),
            jax.ShapeDtypeStruct((heads, 1, rows), f32),
        ],
        compiler_params=params,
        cost_estimate=pl.CostEstimate(
            flops=8 * HD * pairs, bytes_accessed=8 * rows * heads * HD, transcendentals=pairs
        ),
        name="attend",
    )(info, *kv_args)

    moving = nn(attn, cuts[1 % n]).astype(bf16)
    for r in range(n - 1):
        arrived = lax.ppermute(moving, "head", ring)
        summed = arrived.astype(f32) + nn(attn, cuts[(r + 2) % n])
        moving = summed.astype(bf16)
    out_share = moving

    acc = nt(shares[0], cuts[0])
    for r in range(1, n):
        acc = acc + nt(shares[r], cuts[r])
    position = jnp.arange(rows, dtype=jnp.int32)
    valid = (position < rows_p + resp_len[0]).astype(f32)
    dout = (acc * valid[:, None]).astype(bf16)

    parts = []
    half = max(n // 2, 1)
    for first in range(0, n, half):
        part = jnp.concatenate([tn(attn, shares[r]).astype(bf16) for r in range(first, first + half)], 0)
        parts.append(lax.psum(part, TOKENS))
    weight_sum = jnp.zeros(out_weight.shape, f32)
    for r in range(n):
        part = parts[r // half]
        block = lax.slice_in_dim(part, (r % half) * heads * HD, (r % half + 1) * heads * HD, axis=0)
        weight_sum = lax.dynamic_update_slice_in_dim(
            weight_sum, block.astype(f32), lax.rem(z - r + n, n) * share, 1
        )

    acc_specs = [
        k_spec(prompt_len), k_spec(prompt_len), k_spec(prompt_len), k_spec(prompt_len),
        k_spec(rows_r), k_spec(rows_r),
    ]
    wide = jax.ShapeDtypeStruct((prompt_len, kv), f32)
    dpq, drq, dpk, dpv, dsk, dsv, drk, drv = pl.pallas_call(
        functools.partial(backward_kernel, q_group),
        grid=(heads,),
        in_specs=[smem] + kv_specs + [q_spec(rows), q_spec(rows), lse_spec],
        out_specs=[q_spec(rows_p), q_spec(rows_r)] + acc_specs,
        out_shape=[
            jax.ShapeDtypeStruct(prefix_q.shape, bf16),
            jax.ShapeDtypeStruct(resp_q.shape, bf16),
            wide, wide, wide, wide,
            jax.ShapeDtypeStruct(resp_k.shape, bf16),
            jax.ShapeDtypeStruct(resp_v.shape, bf16),
        ],
        scratch_shapes=[pltpu.VMEM((prompt_len, HD), f32)] * 4 + [pltpu.VMEM((rows_r, HD), f32)] * 2,
        compiler_params=params,
        cost_estimate=pl.CostEstimate(
            flops=20 * HD * pairs, bytes_accessed=16 * rows * heads * HD, transcendentals=pairs
        ),
        name="attend_back",
    )(info, *kv_args, attn, dout, lse)

    own_part = jnp.concatenate([dpk, dpv], 1)
    seen_part = jnp.concatenate([dsk, dsv], 1)
    prompts = jnp.arange(2, dtype=jnp.int32)[:, None, None]
    spread = jnp.where(prompts == own, own_part[None], 0.0) + jnp.where(
        prompts == resp_prompt[0], seen_part[None], 0.0
    )
    kv_sum = lax.psum_scatter(
        spread.reshape(2 * prompt_len, 2 * kv).astype(bf16), TOKENS, scatter_dimension=0, tiled=True
    )
    return (
        out_share[:rows_p], out_share[rows_p:],
        dpq, kv_sum[:, :kv].astype(bf16), kv_sum[:, kv:].astype(bf16),
        drq, drk, drv, weight_sum,
    )


def solution(mesh):
    tok = P(TOKENS, "head")
    in_specs = (tok,) * 6 + (P(TOKENS), P(TOKENS), P("head", None), tok, tok)
    out_specs = (tok,) * 8 + (P("head", None),)
    return jax.shard_map(
        on_device, mesh=mesh, in_specs=in_specs, out_specs=out_specs, check_vma=False
    )
```

```python
import functools

import jax
import jax.numpy as jnp
import numpy as np
from jax import lax
from jax.experimental import pallas as pl
from jax.experimental.pallas import tpu as pltpu
from jax.sharding import PartitionSpec as P

HD = 128
TOKENS = ("group", "seq")
SCALE = HD ** (-0.5)
LOG2E = 1.4426950408889634
MASKED = -1e30


def nt(a, b):
    return lax.dot_general(a, b, (((1,), (1,)), ((), ())), preferred_element_type=jnp.float32)


def tn(a, b):
    return lax.dot_general(a, b, (((0,), (0,)), ((), ())), preferred_element_type=jnp.float32)


def nn(a, b):
    return jnp.dot(a, b, preferred_element_type=jnp.float32)


def causal_t(scores, offset):
    key = lax.broadcasted_iota(jnp.int32, scores.shape, 0)
    row = lax.broadcasted_iota(jnp.int32, scores.shape, 1)
    return jnp.where(key <= row + offset, scores, MASKED)


def forward_kernel(info, pq, rq, pk, pv, sk, sv, rk, rv, attn, lse):
    rows_p = pq.shape[0]
    factor = SCALE * LOG2E
    s = causal_t(nt(pk[...], pq[...]), info[0])
    top = jnp.max(s, 0, keepdims=True)
    p = jnp.exp2((s - top) * factor)
    total = jnp.sum(p, 0, keepdims=True)
    out = tn(pv[...], p.astype(jnp.bfloat16)) / total
    attn[:rows_p] = out.T.astype(jnp.bfloat16)
    lse[0, :, :rows_p] = top * factor + jnp.log2(total)
    a = nt(sk[...], rq[...])
    b = causal_t(nt(rk[...], rq[...]), 0)
    top = jnp.maximum(jnp.max(a, 0, keepdims=True), jnp.max(b, 0, keepdims=True))
    pa = jnp.exp2((a - top) * factor)
    pb = jnp.exp2((b - top) * factor)
    total = jnp.sum(pa, 0, keepdims=True) + jnp.sum(pb, 0, keepdims=True)
    out = tn(sv[...], pa.astype(jnp.bfloat16)) + tn(rv[...], pb.astype(jnp.bfloat16))
    live = lax.broadcasted_iota(jnp.int32, total.shape, 1) < info[1]
    out = out * jnp.where(live, 1.0 / total, 0.0)
    attn[rows_p:] = out.T.astype(jnp.bfloat16)
    lse[0, :, rows_p:] = top * factor + jnp.log2(total)


def row_sums_t(x):
    high = x.astype(jnp.bfloat16)
    low = (x - high.astype(jnp.float32)).astype(jnp.bfloat16)
    ones = jnp.ones((8, x.shape[1]), jnp.bfloat16)
    return (nt(ones, high) + nt(ones, low))[:1]


def backward_kernel(
    q_group, info, pq, rq, pk, pv, sk, sv, rk, rv, attn, dout, lse,
    dpq, drq, dpk, dpv, dsk, dsv, drk, drv,
    apk, apv, ask, asv, ark, arv,
):
    rows_p = pq.shape[0]
    factor = SCALE * LOG2E
    step = lax.rem(pl.program_id(0), q_group)
    accs = (apk, apv, ask, asv, ark, arv)

    @pl.when(step == 0)
    def _():
        for acc in accs:
            acc[...] = jnp.zeros_like(acc)

    delta = row_sums_t(dout[...].astype(jnp.float32) * attn[...].astype(jnp.float32))

    def piece(q, do, k, v, lse_row, delta_row, offset, acc_k, acc_v):
        s = nt(k, q)
        if offset is not None:
            s = causal_t(s, offset)
        p = jnp.exp2(s * factor - lse_row)
        ds = (p * (nt(v, do) - delta_row)).astype(jnp.bfloat16)
        acc_k[...] += nn(ds, q)
        acc_v[...] += nn(p.astype(jnp.bfloat16), do)
        return tn(k, ds)

    dq = piece(pq[...], dout[:rows_p], pk[...], pv[...], lse[0, :, :rows_p], delta[:, :rows_p],
               info[0], apk, apv)
    dpq[...] = (dq * SCALE).T.astype(jnp.bfloat16)
    q, do, lr, dr = rq[...], dout[rows_p:], lse[0, :, rows_p:], delta[:, rows_p:]
    dq = piece(q, do, sk[...], sv[...], lr, dr, None, ask, asv)
    dq = dq + piece(q, do, rk[...], rv[...], lr, dr, 0, ark, arv)
    drq[...] = (dq * SCALE).T.astype(jnp.bfloat16)

    @pl.when(step == q_group - 1)
    def _():
        dpk[...] = apk[...] * SCALE
        dpv[...] = apv[...]
        dsk[...] = ask[...] * SCALE
        dsv[...] = asv[...]
        drk[...] = (ark[...] * SCALE).astype(jnp.bfloat16)
        drv[...] = arv[...].astype(jnp.bfloat16)


def token_bits():
    bits = []
    for axis in ("group", "seq"):
        weight = 1
        while weight < lax.axis_size(axis):
            digit = lax.rem(lax.axis_index(axis) // weight, 2)
            bits.append((axis, weight, digit))
            weight *= 2
    return bits


def swap(x, bit):
    axis, weight, _ = bit
    size = lax.axis_size(axis)
    return lax.ppermute(x, axis, [(i, i ^ weight) for i in range(size)])


def scatter_sum(x, bits):
    for bit in bits:
        half = x.shape[0] // 2
        kept = lax.dynamic_slice_in_dim(x, bit[2] * half, half, 0)
        sent = lax.dynamic_slice_in_dim(x, (1 - bit[2]) * half, half, 0)
        got = swap(sent, bit)
        x = (kept.astype(jnp.float32) + got.astype(jnp.float32)).astype(jnp.bfloat16)
    return x


def gather_rows(x, bits):
    for bit in bits:
        got = swap(x, bit)
        first = bit[2] == 0
        x = jnp.concatenate([jnp.where(first, x, got), jnp.where(first, got, x)], 0)
    return x


def orders(bits):
    inner = [b for b in bits if b[0] == "seq"]
    outer = [b for b in bits if b[0] == "group"]
    return inner, outer, outer[::-1]


def all_sum(x):
    inner, one, two = orders(token_bits())
    half = x.shape[0] // 2
    out = []
    for part, outer in ((x[:half], one), (x[half:], two)):
        path = inner + outer
        out.append(gather_rows(scatter_sum(part, path), path[::-1]))
    return jnp.concatenate(out, 0)


def natural_digits():
    return [b[:2] for b in token_bits()[::-1] if b[0] == "group"] + [
        b[:2] for b in token_bits()[::-1] if b[0] == "seq"
    ]


def reorder(x, origins, axes):
    names = [b[:2] for b in origins]
    order = [names.index(b[:2]) for b in axes]
    places = np.arange(2 ** len(names)).reshape((2,) * len(names)).transpose(order).reshape(-1)
    block = x.shape[0] // len(places)
    return jnp.concatenate([x[p * block:(p + 1) * block] for p in places.tolist()], 0)


def owner_rows(x, path):
    return reorder(x, natural_digits(), path)


def natural_rows(x, path):
    return reorder(x, path, natural_digits())


def token_gather(x, outer, inner):
    path = inner + outer
    return natural_rows(gather_rows(x, path[::-1]), path)


def token_scatter(x, outer, inner):
    path = inner + outer
    return scatter_sum(owner_rows(x, path), path)


def on_device(
    prefix_q, prefix_k, prefix_v, resp_q, resp_k, resp_v,
    resp_len, resp_prompt, out_weight, prefix_grad, resp_grad,
):
    n = lax.axis_size("head")
    z = lax.axis_index("head")
    shards = lax.axis_size(TOKENS)
    me = lax.axis_index(TOKENS)
    rows_p, rows_r = prefix_q.shape[0], resp_q.shape[0]
    rows = rows_p + rows_r
    kv = prefix_k.shape[1]
    q_group = prefix_q.shape[1] // kv
    heads = prefix_q.shape[1] // HD
    prompt_len = rows_p * shards // 2
    share = prefix_grad.shape[1]
    bf16, f32 = jnp.bfloat16, jnp.float32
    inner, one, two = orders(token_bits())

    mine = jnp.concatenate([prefix_grad, resp_grad], 0)

    def hop(x, low, high, back=False):
        pairs = [(i, i + 1) for i in range(low, high)]
        return lax.ppermute(x, "head", [(j, i) for i, j in pairs] if back else pairs)

    rightward = [mine, hop(mine, 0, n - 1)]
    leftward = [mine, hop(mine, 0, n - 1, True)]

    def weight_cut(r):
        return lax.dynamic_slice_in_dim(out_weight, lax.rem(z - r + n, n) * share, share, 1)

    cuts = [weight_cut(r) for r in range(n)]

    own = me * rows_p // prompt_len
    all_k = token_gather(prefix_k, one, inner)
    all_v = token_gather(prefix_v, two, inner)
    seen = resp_prompt[0]
    own_k = lax.dynamic_slice_in_dim(all_k, own * prompt_len, prompt_len, 0)
    own_v = lax.dynamic_slice_in_dim(all_v, own * prompt_len, prompt_len, 0)
    seen_k = lax.dynamic_slice_in_dim(all_k, seen * prompt_len, prompt_len, 0)
    seen_v = lax.dynamic_slice_in_dim(all_v, seen * prompt_len, prompt_len, 0)
    info = jnp.stack([me * rows_p - own * prompt_len, resp_len[0]]).astype(jnp.int32)

    smem = pl.BlockSpec(memory_space=pltpu.SMEM)

    def q_spec(count):
        return pl.BlockSpec((count, HD), lambda i: (0, i))

    def k_spec(count):
        return pl.BlockSpec((count, HD), lambda i: (0, i // q_group))

    kv_specs = [
        q_spec(rows_p), q_spec(rows_r),
        k_spec(prompt_len), k_spec(prompt_len),
        k_spec(prompt_len), k_spec(prompt_len),
        k_spec(rows_r), k_spec(rows_r),
    ]
    kv_args = (prefix_q, resp_q, own_k, own_v, seen_k, seen_v, resp_k, resp_v)
    lse_spec = pl.BlockSpec((1, 1, rows), lambda i: (i, 0, 0))
    pairs = heads * (rows_p * prompt_len + rows_r * (prompt_len + rows_r))
    params = pltpu.CompilerParams(
        dimension_semantics=("arbitrary",), vmem_limit_bytes=48 * 2**20
    )
    attn, lse = pl.pallas_call(
        forward_kernel,
        grid=(heads,),
        in_specs=[smem] + kv_specs,
        out_specs=[q_spec(rows), lse_spec],
        out_shape=[
            jax.ShapeDtypeStruct((rows, heads * HD), bf16),
            jax.ShapeDtypeStruct((heads, 1, rows), f32),
        ],
        compiler_params=params,
        cost_estimate=pl.CostEstimate(
            flops=8 * HD * pairs, bytes_accessed=8 * rows * heads * HD, transcendentals=pairs
        ),
        name="attend",
    )(info, *kv_args)

    held = lax.optimization_barrier((attn, rightward[1], leftward[1]))
    attn, rightward[1], leftward[1] = held
    for r in range(2, n):
        rightward.append(hop(rightward[-1], r - 1, n - 1))
        leftward.append(hop(leftward[-1], 0, n - r, True))
    shares = [mine]
    for r in range(1, n):
        shares.append(jnp.where(z >= r, rightward[r], leftward[n - r]))

    terms = [nn(attn, cuts[r]) for r in range(n)]
    sum_r, sum_l = None, None
    for r in range(1, n):
        out_r, out_l = terms[r], terms[n - r]
        if r > 1:
            out_r, out_l = out_r + sum_r.astype(f32), out_l + sum_l.astype(f32)
        sum_r = hop(out_r.astype(bf16), 0, min(r, n - 1))
        sum_l = hop(out_l.astype(bf16), n - 1 - min(r, n - 1), n - 1, True)
    out_share = (terms[0] + sum_r.astype(f32) + sum_l.astype(f32)).astype(bf16)

    acc = nt(shares[0], cuts[0])
    for r in range(1, n):
        acc = acc + nt(shares[r], cuts[r])
    position = jnp.arange(rows, dtype=jnp.int32)
    valid = (position < rows_p + resp_len[0]).astype(f32)
    dout = (acc * valid[:, None]).astype(bf16)

    weight_sum = jnp.zeros(out_weight.shape, f32)
    for r in range(n):
        part = all_sum(tn(attn, shares[r]).astype(bf16))
        weight_sum = lax.dynamic_update_slice_in_dim(
            weight_sum, part.astype(f32), lax.rem(z - r + n, n) * share, 1
        )

    acc_specs = [
        k_spec(prompt_len), k_spec(prompt_len), k_spec(prompt_len), k_spec(prompt_len),
        k_spec(rows_r), k_spec(rows_r),
    ]
    wide = jax.ShapeDtypeStruct((prompt_len, kv), f32)
    dpq, drq, dpk, dpv, dsk, dsv, drk, drv = pl.pallas_call(
        functools.partial(backward_kernel, q_group),
        grid=(heads,),
        in_specs=[smem] + kv_specs + [q_spec(rows), q_spec(rows), lse_spec],
        out_specs=[q_spec(rows_p), q_spec(rows_r)] + acc_specs,
        out_shape=[
            jax.ShapeDtypeStruct(prefix_q.shape, bf16),
            jax.ShapeDtypeStruct(resp_q.shape, bf16),
            wide, wide, wide, wide,
            jax.ShapeDtypeStruct(resp_k.shape, bf16),
            jax.ShapeDtypeStruct(resp_v.shape, bf16),
        ],
        scratch_shapes=[pltpu.VMEM((prompt_len, HD), f32)] * 4 + [pltpu.VMEM((rows_r, HD), f32)] * 2,
        compiler_params=params,
        cost_estimate=pl.CostEstimate(
            flops=20 * HD * pairs, bytes_accessed=16 * rows * heads * HD, transcendentals=pairs
        ),
        name="attend_back",
    )(info, *kv_args, attn, dout, lse)

    prompts = jnp.arange(2, dtype=jnp.int32)[:, None, None]

    def to_owners(own_part, seen_part, outer):
        spread = jnp.where(prompts == own, own_part[None], 0.0)
        spread = spread + jnp.where(prompts == seen, seen_part[None], 0.0)
        return token_scatter(spread.reshape(2 * prompt_len, kv).astype(bf16), outer, inner)

    d_prefix_k = to_owners(dpk, dsk, one)
    d_prefix_v = to_owners(dpv, dsv, two)
    return (
        out_share[:rows_p], out_share[rows_p:],
        dpq, d_prefix_k, d_prefix_v,
        drq, drk, drv, weight_sum,
    )


def solution(mesh):
    tok = P(TOKENS, "head")
    in_specs = (tok,) * 6 + (P(TOKENS), P(TOKENS), P("head", None), tok, tok)
    out_specs = (tok,) * 8 + (P("head", None),)
    return jax.shard_map(
        on_device, mesh=mesh, in_specs=in_specs, out_specs=out_specs, check_vma=False
    )
```

```python
import functools

import jax
import jax.numpy as jnp
import numpy as np
from jax import lax
from jax.experimental import pallas as pl
from jax.experimental.pallas import tpu as pltpu
from jax.sharding import PartitionSpec as P

HD = 128
TOKENS = ("group", "seq")
SCALE = HD ** (-0.5)
LOG2E = 1.4426950408889634
MASKED = -1e30


def nt(a, b):
    return lax.dot_general(a, b, (((1,), (1,)), ((), ())), preferred_element_type=jnp.float32)


def tn(a, b):
    return lax.dot_general(a, b, (((0,), (0,)), ((), ())), preferred_element_type=jnp.float32)


def nn(a, b):
    return jnp.dot(a, b, preferred_element_type=jnp.float32)


def causal_t(scores, offset):
    key = lax.broadcasted_iota(jnp.int32, scores.shape, 0)
    row = lax.broadcasted_iota(jnp.int32, scores.shape, 1)
    return jnp.where(key <= row + offset, scores, MASKED)


def forward_kernel(info, pq, rq, pk, pv, sk, sv, rk, rv, attn, lse):
    rows_p = pq.shape[0]
    factor = SCALE * LOG2E
    s = causal_t(nt(pk[...], pq[...]), info[0])
    top = jnp.max(s, 0, keepdims=True)
    p = jnp.exp2((s - top) * factor)
    total = jnp.sum(p, 0, keepdims=True)
    out = tn(pv[...], p.astype(jnp.bfloat16)) / total
    attn[:rows_p] = out.T.astype(jnp.bfloat16)
    lse[0, :, :rows_p] = top * factor + jnp.log2(total)
    a = nt(sk[...], rq[...])
    b = causal_t(nt(rk[...], rq[...]), 0)
    top = jnp.maximum(jnp.max(a, 0, keepdims=True), jnp.max(b, 0, keepdims=True))
    pa = jnp.exp2((a - top) * factor)
    pb = jnp.exp2((b - top) * factor)
    total = jnp.sum(pa, 0, keepdims=True) + jnp.sum(pb, 0, keepdims=True)
    out = tn(sv[...], pa.astype(jnp.bfloat16)) + tn(rv[...], pb.astype(jnp.bfloat16))
    live = lax.broadcasted_iota(jnp.int32, total.shape, 1) < info[1]
    out = out * jnp.where(live, 1.0 / total, 0.0)
    attn[rows_p:] = out.T.astype(jnp.bfloat16)
    lse[0, :, rows_p:] = top * factor + jnp.log2(total)


def row_sums_t(x):
    high = x.astype(jnp.bfloat16)
    low = (x - high.astype(jnp.float32)).astype(jnp.bfloat16)
    ones = jnp.ones((8, x.shape[1]), jnp.bfloat16)
    return (nt(ones, high) + nt(ones, low))[:1]


def backward_kernel(
    q_group, info, pq, rq, pk, pv, sk, sv, rk, rv, attn, dout, lse,
    dpq, drq, dpk, dpv, dsk, dsv, drk, drv,
    apk, apv, ask, asv, ark, arv,
):
    rows_p = pq.shape[0]
    factor = SCALE * LOG2E
    step = lax.rem(pl.program_id(0), q_group)
    accs = (apk, apv, ask, asv, ark, arv)

    @pl.when(step == 0)
    def _():
        for acc in accs:
            acc[...] = jnp.zeros_like(acc)

    delta = row_sums_t(dout[...].astype(jnp.float32) * attn[...].astype(jnp.float32))

    def piece(q, do, k, v, lse_row, delta_row, offset, acc_k, acc_v):
        s = nt(k, q)
        if offset is not None:
            s = causal_t(s, offset)
        p = jnp.exp2(s * factor - lse_row)
        ds = (p * (nt(v, do) - delta_row)).astype(jnp.bfloat16)
        acc_k[...] += nn(ds, q)
        acc_v[...] += nn(p.astype(jnp.bfloat16), do)
        return tn(k, ds)

    dq = piece(pq[...], dout[:rows_p], pk[...], pv[...], lse[0, :, :rows_p], delta[:, :rows_p],
               info[0], apk, apv)
    dpq[...] = (dq * SCALE).T.astype(jnp.bfloat16)
    q, do, lr, dr = rq[...], dout[rows_p:], lse[0, :, rows_p:], delta[:, rows_p:]
    dq = piece(q, do, sk[...], sv[...], lr, dr, None, ask, asv)
    dq = dq + piece(q, do, rk[...], rv[...], lr, dr, 0, ark, arv)
    drq[...] = (dq * SCALE).T.astype(jnp.bfloat16)

    @pl.when(step == q_group - 1)
    def _():
        dpk[...] = apk[...] * SCALE
        dpv[...] = apv[...]
        dsk[...] = ask[...] * SCALE
        dsv[...] = asv[...]
        drk[...] = (ark[...] * SCALE).astype(jnp.bfloat16)
        drv[...] = arv[...].astype(jnp.bfloat16)


def token_bits():
    bits = []
    for axis in ("group", "seq"):
        weight = 1
        while weight < lax.axis_size(axis):
            digit = lax.rem(lax.axis_index(axis) // weight, 2)
            bits.append((axis, weight, digit))
            weight *= 2
    return bits


def swap(x, bit):
    axis, weight, _ = bit
    size = lax.axis_size(axis)
    return lax.ppermute(x, axis, [(i, i ^ weight) for i in range(size)])


def scatter_sum(x, bits):
    for bit in bits:
        half = x.shape[0] // 2
        kept = lax.dynamic_slice_in_dim(x, bit[2] * half, half, 0)
        sent = lax.dynamic_slice_in_dim(x, (1 - bit[2]) * half, half, 0)
        got = swap(sent, bit)
        x = (kept.astype(jnp.float32) + got.astype(jnp.float32)).astype(jnp.bfloat16)
    return x


def gather_rows(x, bits):
    for bit in bits:
        got = swap(x, bit)
        first = bit[2] == 0
        x = jnp.concatenate([jnp.where(first, x, got), jnp.where(first, got, x)], 0)
    return x


def orders(bits):
    inner = [b for b in bits if b[0] == "seq"]
    outer = [b for b in bits if b[0] == "group"]
    return inner, outer, outer[::-1]


def all_sum(x):
    inner, one, two = orders(token_bits())
    half = x.shape[0] // 2
    out = []
    for part, outer in ((x[:half], one), (x[half:], two)):
        path = inner + outer
        out.append(gather_rows(scatter_sum(part, path), path[::-1]))
    return jnp.concatenate(out, 0)


def natural_digits():
    return [b[:2] for b in token_bits()[::-1] if b[0] == "group"] + [
        b[:2] for b in token_bits()[::-1] if b[0] == "seq"
    ]


def reorder(x, origins, axes):
    names = [b[:2] for b in origins]
    order = [names.index(b[:2]) for b in axes]
    places = np.arange(2 ** len(names)).reshape((2,) * len(names)).transpose(order).reshape(-1)
    block = x.shape[0] // len(places)
    return jnp.concatenate([x[p * block:(p + 1) * block] for p in places.tolist()], 0)


def owner_rows(x, path):
    return reorder(x, natural_digits(), path)


def natural_rows(x, path):
    return reorder(x, path, natural_digits())


def token_gather(x, outer, inner):
    path = inner + outer
    return natural_rows(gather_rows(x, path[::-1]), path)


def token_scatter(x, outer, inner):
    path = inner + outer
    return scatter_sum(owner_rows(x, path), path)


def on_device(
    prefix_q, prefix_k, prefix_v, resp_q, resp_k, resp_v,
    resp_len, resp_prompt, out_weight, prefix_grad, resp_grad,
):
    n = lax.axis_size("head")
    z = lax.axis_index("head")
    shards = lax.axis_size(TOKENS)
    me = lax.axis_index(TOKENS)
    rows_p, rows_r = prefix_q.shape[0], resp_q.shape[0]
    rows = rows_p + rows_r
    kv = prefix_k.shape[1]
    q_group = prefix_q.shape[1] // kv
    heads = prefix_q.shape[1] // HD
    prompt_len = rows_p * shards // 2
    share = prefix_grad.shape[1]
    bf16, f32 = jnp.bfloat16, jnp.float32
    inner, one, two = orders(token_bits())

    mine = jnp.concatenate([prefix_grad, resp_grad], 0)

    def hop(x, low, high, back=False):
        pairs = [(i, i + 1) for i in range(low, high)]
        return lax.ppermute(x, "head", [(j, i) for i, j in pairs] if back else pairs)

    rightward = [mine, hop(mine, 0, n - 1)]
    leftward = [mine, hop(mine, 0, n - 1, True)]

    def weight_cut(r):
        return lax.dynamic_slice_in_dim(out_weight, lax.rem(z - r + n, n) * share, share, 1)

    cuts = [weight_cut(r) for r in range(n)]

    own = me * rows_p // prompt_len
    all_k = token_gather(prefix_k, one, inner)
    all_v = token_gather(prefix_v, two, inner)
    seen = resp_prompt[0]
    own_k = lax.dynamic_slice_in_dim(all_k, own * prompt_len, prompt_len, 0)
    own_v = lax.dynamic_slice_in_dim(all_v, own * prompt_len, prompt_len, 0)
    seen_k = lax.dynamic_slice_in_dim(all_k, seen * prompt_len, prompt_len, 0)
    seen_v = lax.dynamic_slice_in_dim(all_v, seen * prompt_len, prompt_len, 0)
    info = jnp.stack([me * rows_p - own * prompt_len, resp_len[0]]).astype(jnp.int32)

    smem = pl.BlockSpec(memory_space=pltpu.SMEM)

    def q_spec(count):
        return pl.BlockSpec((count, HD), lambda i: (0, i))

    def k_spec(count):
        return pl.BlockSpec((count, HD), lambda i: (0, i // q_group))

    kv_specs = [
        q_spec(rows_p), q_spec(rows_r),
        k_spec(prompt_len), k_spec(prompt_len),
        k_spec(prompt_len), k_spec(prompt_len),
        k_spec(rows_r), k_spec(rows_r),
    ]
    kv_args = (prefix_q, resp_q, own_k, own_v, seen_k, seen_v, resp_k, resp_v)
    lse_spec = pl.BlockSpec((1, 1, rows), lambda i: (i, 0, 0))
    pairs = heads * (rows_p * prompt_len + rows_r * (prompt_len + rows_r))
    params = pltpu.CompilerParams(
        dimension_semantics=("arbitrary",), vmem_limit_bytes=48 * 2**20
    )
    attn, lse = pl.pallas_call(
        forward_kernel,
        grid=(heads,),
        in_specs=[smem] + kv_specs,
        out_specs=[q_spec(rows), lse_spec],
        out_shape=[
            jax.ShapeDtypeStruct((rows, heads * HD), bf16),
            jax.ShapeDtypeStruct((heads, 1, rows), f32),
        ],
        compiler_params=params,
        cost_estimate=pl.CostEstimate(
            flops=8 * HD * pairs, bytes_accessed=8 * rows * heads * HD, transcendentals=pairs
        ),
        name="attend",
    )(info, *kv_args)

    fence = lax.optimization_barrier
    terms = [nn(attn, cuts[r]) for r in range(n)]
    out_r, out_l = terms[1].astype(bf16), terms[n - 1].astype(bf16)
    attn, terms, out_r, out_l, rightward[1], leftward[1] = fence(
        (attn, terms, out_r, out_l, rightward[1], leftward[1])
    )

    def arrived(r):
        return jnp.where(z >= r, rightward[r], leftward[n - r])

    acc = jnp.zeros((rows, heads * HD), f32)
    sums = {}
    ready = [0]
    for r in range(1, n):
        sum_r = hop(out_r, 0, min(r, n - 1))
        sum_l = hop(out_l, n - 1 - min(r, n - 1), n - 1, True)
        if r + 1 < n:
            rightward.append(hop(rightward[r], r, n - 1))
            leftward.append(hop(leftward[r], 0, n - 1 - r, True))
        got = [mine if i == 0 else arrived(i) for i in ready]
        part = [tn(attn, share_i).astype(bf16) for share_i in got]
        for i, share_i in zip(ready, got):
            acc = acc + nt(share_i, cuts[i])
        if got:
            sums[r] = (tuple(ready), all_sum(jnp.concatenate(part, 0)))
        ready = [i for i in range(1, n) if max(i, n - i) == r + 1]
        if r + 1 < n:
            live_sums = sums[r][1] if r in sums else jnp.zeros((8, HD), bf16)
            sum_r, sum_l, rightward[r + 1], leftward[r + 1], acc, live_sums = fence(
                (sum_r, sum_l, rightward[r + 1], leftward[r + 1], acc, live_sums)
            )
            if r in sums:
                sums[r] = (sums[r][0], live_sums)
            out_r = (terms[r + 1] + sum_r.astype(f32)).astype(bf16)
            out_l = (terms[n - r - 1] + sum_l.astype(f32)).astype(bf16)
    out_share = (terms[0] + sum_r.astype(f32) + sum_l.astype(f32)).astype(bf16)

    weight_sum = jnp.zeros(out_weight.shape, f32)
    if ready:
        got = [mine if i == 0 else arrived(i) for i in ready]
        for i, share_i in zip(ready, got):
            acc = acc + nt(share_i, cuts[i])
        sums[n] = (tuple(ready), all_sum(jnp.concatenate([tn(attn, g).astype(bf16) for g in got], 0)))
    for places, total in sums.values():
        for k, i in enumerate(places):
            block = total[k * heads * HD:(k + 1) * heads * HD].astype(f32)
            weight_sum = lax.dynamic_update_slice_in_dim(
                weight_sum, block, lax.rem(z - i + n, n) * share, 1
            )

    position = jnp.arange(rows, dtype=jnp.int32)
    valid = (position < rows_p + resp_len[0]).astype(f32)
    dout = (acc * valid[:, None]).astype(bf16)

    acc_specs = [
        k_spec(prompt_len), k_spec(prompt_len), k_spec(prompt_len), k_spec(prompt_len),
        k_spec(rows_r), k_spec(rows_r),
    ]
    wide = jax.ShapeDtypeStruct((prompt_len, kv), f32)
    dpq, drq, dpk, dpv, dsk, dsv, drk, drv = pl.pallas_call(
        functools.partial(backward_kernel, q_group),
        grid=(heads,),
        in_specs=[smem] + kv_specs + [q_spec(rows), q_spec(rows), lse_spec],
        out_specs=[q_spec(rows_p), q_spec(rows_r)] + acc_specs,
        out_shape=[
            jax.ShapeDtypeStruct(prefix_q.shape, bf16),
            jax.ShapeDtypeStruct(resp_q.shape, bf16),
            wide, wide, wide, wide,
            jax.ShapeDtypeStruct(resp_k.shape, bf16),
            jax.ShapeDtypeStruct(resp_v.shape, bf16),
        ],
        scratch_shapes=[pltpu.VMEM((prompt_len, HD), f32)] * 4 + [pltpu.VMEM((rows_r, HD), f32)] * 2,
        compiler_params=params,
        cost_estimate=pl.CostEstimate(
            flops=20 * HD * pairs, bytes_accessed=16 * rows * heads * HD, transcendentals=pairs
        ),
        name="attend_back",
    )(info, *kv_args, attn, dout, lse)

    prompts = jnp.arange(2, dtype=jnp.int32)[:, None, None]

    def to_owners(own_part, seen_part, outer):
        spread = jnp.where(prompts == own, own_part[None], 0.0)
        spread = spread + jnp.where(prompts == seen, seen_part[None], 0.0)
        return token_scatter(spread.reshape(2 * prompt_len, kv).astype(bf16), outer, inner)

    d_prefix_k = to_owners(dpk, dsk, one)
    d_prefix_v = to_owners(dpv, dsv, two)
    return (
        out_share[:rows_p], out_share[rows_p:],
        dpq, d_prefix_k, d_prefix_v,
        drq, drk, drv, weight_sum,
    )


def solution(mesh):
    tok = P(TOKENS, "head")
    in_specs = (tok,) * 6 + (P(TOKENS), P(TOKENS), P("head", None), tok, tok)
    out_specs = (tok,) * 8 + (P("head", None),)
    return jax.shard_map(
        on_device, mesh=mesh, in_specs=in_specs, out_specs=out_specs, check_vma=False
    )
```
